256 devices in a mesh: gz: 2 (over core), row: 4 (over x), col: 32 (over z, y).
Axes of the slice: x: 4, y: 4, z: 8, core: 2. Of those that a mesh axis runs over, the one named last changes fastest.
Arguments:
- front_matrix: float32 [4096, 4096], P('row', 'col'), may hold values from -6 to 6
- l_panels: float32 [2, 8, 4, 512, 256], P('gz', None, 'row', 'col'), may hold values from -6 to 6
- l_map: int32 [2, 8, 4, 512], P('gz', None, 'row'), may hold values from 0 to 1024, as said below
- u_panels: float32 [2, 8, 32, 64, 256], P('gz', None, 'col', 'row'), may hold values from -0.375 to 0.375
- u_map: int32 [2, 8, 32, 64], P('gz', None, 'col'), may hold values from 0 to 128, as said below
Outputs:
- updated_front: float32 [4096, 4096], P('row', 'col')
The draws below stay inside these ranges and needn't reach their ends.
Inputs may be any that keep to these rules, and one draw needn't show every extreme that they name: l_map[z,h,p,:] lists distinct rows of row block p updated by child h of layer z, used slots first, listed block of 128 rows by block, at most 64 rows to a block; unused slots hold 1024; in every child some row block uses all 512 slots. u_map[z,h,q,:] lists distinct columns of column block q updated by child h of layer z, used slots first, listed block of 128 columns by block, at most 64 to a block; unused slots hold 128; in every child some column block uses all 64 slots.
All inputs are finite; a program needn't handle non-finite values.
Results may differ from the reference program's by a relative error of at most 0.0001.
Values sent between devices are 32-bit elements; how exact they have to be, the bound alone decides.
A program may use at most 64 MiB of HBM per device.

```python
import jax
import jax.numpy as jnp
from jax import lax

F = 4096
K = 256
TILE = 128
HT = 64
NCH = 8
NL = 2
FT = 32
FR = 1024
FC = 128
TPR = 8
TPC = 1
RL = 512
RU = 64
N_ROW = 4
N_COL = 32


def index_sets(key):
    key_counts, key_rowfull, key_colfull, key_places = jax.random.split(key, 4)
    counts = jax.random.randint(key_counts, (NL, NCH, FT), HT // 4, HT + 1)
    full_row = jax.random.randint(key_rowfull, (NL, NCH, 1), 0, FT // TPR)
    full_col = jax.random.randint(key_colfull, (NL, NCH, 1), 0, FT // TPC)
    tile_ids = jnp.arange(FT, dtype=jnp.int32)[None, None, :]
    forced = (tile_ids // TPR == full_row) | (tile_ids // TPC == full_col)
    counts = jnp.where(forced, HT, counts)
    subkeys = jax.random.split(key_places, NL * NCH * FT)
    positions = jax.vmap(lambda single: jax.random.permutation(single, TILE))(subkeys)
    positions = positions.reshape(NL, NCH, FT, TILE).astype(jnp.int32)
    is_used = jnp.arange(TILE, dtype=jnp.int32)[None, None, None, :] < counts[..., None]
    return (positions, is_used)


def compact(positions, is_used, per_group, slots, width):
    group_count = FT // per_group
    span = per_group * TILE
    within = positions.reshape(NL, NCH, group_count, span)
    within = within + jnp.arange(span, dtype=jnp.int32) // TILE * TILE
    used = is_used.reshape(NL, NCH, group_count, span)
    slot_ids = jnp.arange(span, dtype=jnp.int32)
    ranked = jnp.where(used, slot_ids, slot_ids + span)
    ranking = jnp.argsort(ranked, axis=-1)[..., :slots]
    picked = jnp.take_along_axis(within, ranking, axis=-1)
    kept = jnp.take_along_axis(used, ranking, axis=-1)
    return jnp.where(kept, picked, width).astype(jnp.int32)


def draw_l_map(key, part):
    positions, is_used = index_sets(jax.random.fold_in(key, 11))
    return compact(positions, is_used, TPR, RL, FR)


def draw_u_map(key, part):
    positions, is_used = index_sets(jax.random.fold_in(key, 12))
    return compact(positions, is_used, TPC, RU, FC)


def block_scale(key, dims, shards, smallest, high):
    def one(axis_at, blocks):
        steps = jax.random.uniform(jax.random.fold_in(jax.random.fold_in(key, 6), axis_at), (blocks,), jnp.float32, smallest / len(shards), high / len(shards))
        return jnp.repeat(jnp.exp(steps), dims[axis_at] // blocks).reshape((-1,) + (1,) * (len(dims) - axis_at - 1))

    factor_of = one(*shards[0])
    for cut in shards[1:]:
        factor_of = factor_of * one(*cut)
    return factor_of


def centred(own_key, extent, scale, limit, shards=(), held_as=jnp.bfloat16):
    drawn = scale * jax.random.normal(own_key, extent, jnp.float32)
    if shards:
        drawn = drawn * block_scale(own_key, extent, shards, -0.22, 0.18)
    return jnp.clip(drawn, -limit, limit).astype(held_as)


def setup_inputs(seed: int = 0) -> dict:
    key_list = jax.random.split(jax.random.key(seed), 6)
    front_matrix = centred(key_list[0], (F, F), 1.0, 6.0, ((0, 4), (1, 32)), jnp.float32)
    l_panels = centred(key_list[1], (NL, NCH, N_ROW, RL, K), 1.0, 6.0, ((0, 2), (2, 4), (3, 32)), jnp.float32)
    l_map = draw_l_map(jax.random.fold_in(key_list[5], 71), 0)
    u_panels = centred(key_list[3], (NL, NCH, N_COL, RU, K), K ** -0.5, 0.375, ((0, 2), (2, 32), (3, 4)), jnp.float32)
    u_map = draw_u_map(jax.random.fold_in(key_list[5], 71), 0)
    return {"front_matrix": front_matrix, "l_panels": l_panels, "l_map": l_map, "u_panels": u_panels, "u_map": u_map}


def reference(front_matrix, l_panels, l_map, u_panels, u_map):
    update = jnp.zeros((F, F), jnp.float32)
    for layer_idx in range(NL):
        for child_idx in range(NCH):
            row_map = l_map[layer_idx, child_idx]
            col_map = u_map[layer_idx, child_idx]
            row_base = jnp.arange(N_ROW, dtype=jnp.int32)[:, None] * FR
            col_base = jnp.arange(N_COL, dtype=jnp.int32)[:, None] * FC
            row_index = jnp.where(row_map < FR, row_base + row_map, F).reshape(-1)
            col_index = jnp.where(col_map < FC, col_base + col_map, F).reshape(-1)
            left_panel = l_panels[layer_idx, child_idx].reshape(N_ROW * RL, K)
            right_panel = u_panels[layer_idx, child_idx].reshape(N_COL * RU, K)
            products = jnp.dot(left_panel, right_panel.T, precision=lax.Precision.HIGHEST, preferred_element_type=jnp.float32)
            update = update.at[row_index[:, None], col_index[None, :]].add(products, mode="drop")
    return front_matrix - update
```

```python
import functools

import jax
import jax.numpy as jnp
from jax import lax
from jax.experimental import pallas as pl
from jax.experimental.pallas import tpu as pltpu
from jax.sharding import PartitionSpec as P

MESH = pl.DeviceIdType.MESH
F32 = jnp.float32
BF16 = jnp.bfloat16
NX, NY, NZ = 4, 4, 8
GROUPS = ((0, 1), (2, 7), (6, 3), (4, 5))
CHUNKS = 4


def split(value):
    high = value.astype(BF16)
    return high, (value - high.astype(F32)).astype(BF16)


def dot_nt(left, right):
    return lax.dot_general(left, right, (((1,), (1,)), ((), ())), preferred_element_type=F32)


def kernel(
    front, l_in, lmap, u_in, umap, out,
    lbuf, ubuf, whi, wlo, hot, col_hot, packed, recv, dense, acc, mine, other, front_v,
    uy_s, uy_r, ux_s, ux_r, ly_s, ly_r, zm_s, zp_s, z_r, res_s, res_r, ex_s, ex_r, loc,
):
    core, x, col = lax.axis_index("gz"), lax.axis_index("row"), lax.axis_index("col")
    y, z = lax.rem(col, NY), lax.div(col, NY)
    peer_y = [lax.rem(y + d, NY) for d in range(NY)]
    from_y = [lax.rem(y + NY - d, NY) for d in range(NY)]

    def at_y(d):
        return (core, x, z * NY + peer_y[d])

    def at_x(d):
        return (core, lax.rem(x + d, NX), col)

    def at_z(d):
        return (core, x, lax.rem(z + NZ + d, NZ) * NY + y)

    twin = (1 - core, x, col)
    peers = [at_y(d) for d in (1, 2, 3)] + [at_x(d) for d in (1, 2, 3)] + [at_z(1), at_z(-1), twin]
    barrier = pltpu.get_barrier_semaphore()
    for peer in peers:
        pl.semaphore_signal(barrier, inc=1, device_id=peer, device_id_type=MESH)
    fetch = pltpu.make_async_copy(front, front_v, loc.at[0])
    own_l = pltpu.make_async_copy(l_in.at[0, pl.ds(2 * y, 2), 0], lbuf.at[0, y], loc.at[1])
    own_u = pltpu.make_async_copy(u_in.at[0, pl.ds(2 * y, 2), 0], ubuf.at[x, y], loc.at[2])
    fetch.start()
    own_l.start()
    own_u.start()
    pl.semaphore_wait(barrier, len(peers))

    sent = []

    def send(src, dst, send_sem, recv_sem, device):
        copy = pltpu.make_async_remote_copy(
            src_ref=src, dst_ref=dst, send_sem=send_sem, recv_sem=recv_sem,
            device_id=device, device_id_type=MESH,
        )
        copy.start()
        sent.append(copy)
        return copy

    u_y, u_x, l_y = {}, {}, {}
    for d in (1, 3, 2):
        u_y[d] = send(
            u_in.at[0, pl.ds(2 * peer_y[d], 2), 0], ubuf.at[x, y], uy_s.at[d - 1], uy_r.at[d - 1], at_y(d)
        )
    for d in (1, 3, 2):
        u_x[d, 0] = send(
            u_in.at[0, pl.ds(2 * y, 2), 0], ubuf.at[x, y], ux_s.at[d - 1, 0], ux_r.at[d - 1, 0], at_x(d)
        )
    for d in (1, 3, 2):
        l_y[d] = send(
            l_in.at[0, pl.ds(2 * peer_y[d], 2), 0], lbuf.at[0, y], ly_s.at[d - 1], ly_r.at[d - 1], at_y(d)
        )

    zc = {}

    def z_send(rel, k, down, src=None):
        piece = from_y[k]
        src = lbuf.at[rel, piece] if src is None else src
        if down:
            to = rel + 1
            zc[to, k] = send(src, lbuf.at[to, piece], zm_s.at[rel, k], z_r.at[to, k], at_z(-1))
        else:
            to = (rel + NZ - 1) % NZ
            zc[to, k] = send(src, lbuf.at[to, piece], zp_s.at[rel, k], z_r.at[to, k], at_z(1))

    z_send(0, 0, True, l_in.at[0, pl.ds(2 * y, 2), 0])
    z_send(0, 0, False, l_in.at[0, pl.ds(2 * y, 2), 0])

    def z_pass(rel):
        for k in range(NY):
            zc[rel, k].wait_recv()
            if rel in (1, 2) or (rel == 3 and k < 2):
                z_send(rel, k, True)
            if rel in (7, 6) or (rel == 5 and k >= 2):
                z_send(rel, k, False)

    lane = lax.broadcasted_iota(jnp.int32, (1, 128), 1)

    col_ids = lax.broadcasted_iota(jnp.int32, (256, 128), 0)
    for h in range(8):
        single = umap[0, h]
        both = jnp.concatenate([single, single], axis=1)
        target = jnp.where(lane < 64, jnp.where(both < 128, both, -1), both + 128)
        col_hot[h] = (col_ids == target).astype(F32).astype(BF16)

    for d in (1, 3, 2):
        u_y[d].wait_recv()
        for dx in (1, 3, 2):
            piece = ubuf.at[x, from_y[d]]
            u_x[dx, d] = send(piece, piece, ux_s.at[dx - 1, d], ux_r.at[dx - 1, d], at_x(dx))
    for d in (1, 3, 2):
        l_y[d].wait_recv()
        z_send(0, d, True)
        z_send(0, d, False)

    shift = lax.rem(NZ - z, NZ) * 64

    def row_hots(tiles):
        for tile in tiles:
            d, c = divmod(tile, 2)
            turned = pltpu.roll(lmap[0, 2 * from_y[d] + c], shift, 1)
            t = [turned[:, 128 * i : 128 * i + 128] for i in range(4)]
            rows = (t[0], jnp.where(lane < 64, t[1], t[3]), jnp.where(lane < 64, t[3], t[1]), t[2])

            def fill(step, carry):
                base = pl.multiple_of(step * 64, 64)
                ids = lax.broadcasted_iota(jnp.int32, (64, 128), 0) + base
                for g in range(4):
                    hot[g, pl.ds(base, 64), tile * 128 : tile * 128 + 128] = (
                        (ids == rows[g]).astype(F32).astype(BF16)
                    )
                return carry

            lax.fori_loop(0, 16, fill, 0)

    row_hots((0, 1, 2, 3))
    z_pass(1)
    z_pass(7)
    row_hots((4, 5, 6, 7))

    own_u.wait()
    for k in range(NY):
        for dx in (1, 3, 2):
            u_x[dx, k].wait_recv()
    for c in range(2):
        for q in range(NY):
            high, low = split(ubuf[:, q, c].reshape(64, 256))
            whi[c, 64 * q : 64 * q + 64] = high
            wlo[c, 64 * q : 64 * q + 64] = low
    own_l.wait()

    rc = {}

    def multiply(g):
        first, second = GROUPS[g]
        for c in range(2):
            left = jnp.concatenate(
                [lbuf[first, :, c].reshape(64, 256), lbuf[second, :, c].reshape(64, 256)], axis=0
            )
            high, low = split(left)
            prod = dot_nt(high, wlo[c]) + dot_nt(low, whi[c]) + dot_nt(high, whi[c])
            for j in range(2):
                top = prod[:64, 128 * j : 128 * j + 128]
                bottom = prod[64:, 128 * j : 128 * j + 128]
                packed[g, c, 2 * j] = jnp.where(lane < 64, top, pltpu.roll(bottom, 64, 1))
                packed[g, c, 2 * j + 1] = jnp.where(lane < 64, pltpu.roll(top, 64, 1), bottom)
            for d in (2, 1, 3):
                rc[g, c, d] = send(
                    packed.at[g, c, peer_y[d]], recv.at[g, c, d - 1],
                    res_s.at[g, c, d - 1], res_r.at[g, c, d - 1], at_y(d),
                )

    def expand(g):
        for d in (0, 1, 3, 2):
            for c in range(2):
                if d == 0:
                    value = packed[g, c, y]
                else:
                    rc[g, c, d].wait_recv()
                    value = recv[g, c, d - 1]
                high, low = split(value)
                wide = dot_nt(jnp.concatenate([high, low], axis=0), col_hot[2 * from_y[d] + c]).astype(BF16)
                at = (2 * d + c) * 128
                dense[at : at + 64, :128] = wide[:64, :128]
                dense[at + 64 : at + 128, :128] = wide[:64, 128:]
                dense[at : at + 64, 128:] = wide[64:, :128]
                dense[at + 64 : at + 128, 128:] = wide[64:, 128:]

    size = 1024 // CHUNKS

    def scatter(g, chunk):
        rows = slice(chunk * size, chunk * size + size)
        both = jnp.dot(hot[g, rows], dense[...], preferred_element_type=F32)
        return both[:, :128] + both[:, 128:]

    multiply(0)
    z_pass(2)
    z_pass(6)
    multiply(1)
    z_pass(3)
    z_pass(5)
    multiply(2)
    z_pass(4)
    multiply(3)

    for g in range(3):
        expand(g)
        for chunk in range(CHUNKS):
            rows = slice(chunk * size, chunk * size + size)
            part = scatter(g, chunk)
            acc[rows] = part if g == 0 else acc[rows] + part
    expand(3)
    ex = []
    for chunk in range(CHUNKS):
        rows = slice(chunk * size, chunk * size + size)
        mine[rows] = acc[rows] + scatter(3, chunk)
        ex.append(send(mine.at[rows], other.at[rows], ex_s.at[chunk], ex_r.at[chunk], twin))
    fetch.wait()
    for chunk in range(CHUNKS):
        rows = slice(chunk * size, chunk * size + size)
        ex[chunk].wait_recv()
        out[rows] = front_v[rows] - (mine[rows] + other[rows])
    for copy in sent:
        copy.wait_send()


def shards(front_matrix, l_panels, l_map, u_panels, u_map):
    hbm = pl.BlockSpec(memory_space=pltpu.HBM)
    vmem = pl.BlockSpec(memory_space=pltpu.VMEM)
    dma = pltpu.SemaphoreType.DMA
    return pl.pallas_call(
        kernel,
        out_shape=jax.ShapeDtypeStruct((1024, 128), F32),
        in_specs=[hbm, hbm, vmem, hbm, vmem],
        out_specs=vmem,
        scratch_shapes=[
            pltpu.VMEM((NZ, NY, 2, 16, 256), F32),
            pltpu.VMEM((NX, NY, 2, 16, 256), F32),
            pltpu.VMEM((2, 256, 256), BF16),
            pltpu.VMEM((2, 256, 256), BF16),
            pltpu.VMEM((4, 1024, 1024), BF16),
            pltpu.VMEM((8, 256, 128), BF16),
            pltpu.VMEM((4, 2, NY, 64, 128), F32),
            pltpu.VMEM((4, 2, 3, 64, 128), F32),
            pltpu.VMEM((1024, 256), BF16),
            pltpu.VMEM((1024, 128), F32),
            pltpu.VMEM((1024, 128), F32),
            pltpu.VMEM((1024, 128), F32),
            pltpu.VMEM((1024, 128), F32),
            dma((3,)), dma((3,)), dma((3, 4)), dma((3, 4)), dma((3,)), dma((3,)),
            dma((NZ, 4)), dma((NZ, 4)), dma((NZ, 4)),
            dma((4, 2, 3)), dma((4, 2, 3)), dma((CHUNKS,)), dma((CHUNKS,)), dma((3,)),
        ],
        compiler_params=pltpu.CompilerParams(
            collective_id=0, has_side_effects=True, vmem_limit_bytes=48 << 20
        ),
        name="extend_add",
    )(front_matrix, l_panels, l_map, u_panels, u_map)


def solution(mesh):
    placed = (
        P("row", "col"),
        P("gz", None, "row", "col", None),
        P("gz", None, "row", None),
        P("gz", None, "col", "row", None),
        P("gz", None, "col", None),
    )
    return jax.shard_map(
        shards, mesh=mesh, in_specs=placed, out_specs=P("row", "col"), check_vma=False
    )
```

```python
import functools

import jax
import jax.numpy as jnp
from jax import lax
from jax.experimental import pallas as pl
from jax.experimental.pallas import tpu as pltpu
from jax.sharding import PartitionSpec as P

MESH = pl.DeviceIdType.MESH
F32 = jnp.float32
BF16 = jnp.bfloat16
NX, NY, NZ = 4, 4, 8
GROUPS = ((0, 1), (2, 7), (6, 3), (4, 5))
CHUNKS = 4


def split(value):
    high = value.astype(BF16)
    return high, (value - high.astype(F32)).astype(BF16)


def dot_nt(left, right):
    return lax.dot_general(left, right, (((1,), (1,)), ((), ())), preferred_element_type=F32)


def kernel(
    front, l_in, lmap_in, u_in, umap_in, out,
    lbuf, ubuf, whi, wlo, hot, col_hot, packed, recv, dense, acc, mine, other, front_v, lmap, umap,
    uy_s, uy_r, ux_s, ux_r, ly_s, zm_s, zp_s, z_r, res_s, res_r, ex_s, ex_r, loc,
):
    core, x, col = lax.axis_index("gz"), lax.axis_index("row"), lax.axis_index("col")
    y, z = lax.rem(col, NY), lax.div(col, NY)
    peer_y = [lax.rem(y + d, NY) for d in range(NY)]
    from_y = [lax.rem(y + NY - d, NY) for d in range(NY)]

    def at_y(d):
        return (core, x, z * NY + peer_y[d])

    def at_x(d):
        return (core, lax.rem(x + d, NX), col)

    def at_z(d, dy=0):
        return (core, x, lax.rem(z + NZ + d, NZ) * NY + peer_y[dy])

    twin = (1 - core, x, col)
    peers = [at_y(d) for d in (1, 2, 3)] + [at_x(d) for d in (1, 2, 3)] + [twin]
    peers += [at_z(d, dy) for d in (1, -1) for dy in range(NY)]
    barrier = pltpu.get_barrier_semaphore()
    for peer in peers:
        pl.semaphore_signal(barrier, inc=1, device_id=peer, device_id_type=MESH)
    fetch = pltpu.make_async_copy(front, front_v, loc.at[0])
    own_l = pltpu.make_async_copy(l_in.at[0, pl.ds(2 * y, 2), 0], lbuf.at[0, y], loc.at[1])
    maps = (
        pltpu.make_async_copy(lmap_in.at[0], lmap, loc.at[3]),
        pltpu.make_async_copy(umap_in.at[0], umap, loc.at[4]),
    )
    own_u = pltpu.make_async_copy(u_in.at[0, pl.ds(2 * y, 2), 0], ubuf.at[:, x, y], loc.at[2])
    for copy in maps:
        copy.start()
    fetch.start()
    own_l.start()
    own_u.start()
    pl.semaphore_wait(barrier, len(peers))

    sent = []

    def send(src, dst, send_sem, recv_sem, device):
        copy = pltpu.make_async_remote_copy(
            src_ref=src, dst_ref=dst, send_sem=send_sem, recv_sem=recv_sem,
            device_id=device, device_id_type=MESH,
        )
        copy.start()
        sent.append(copy)
        return copy

    u_y, u_x = {}, {}

    def u_spread(c):
        for d in (1, 3, 2):
            u_y[d, c] = send(
                u_in.at[0, 2 * peer_y[d] + c, 0], ubuf.at[c, x, y],
                uy_s.at[d - 1, c], uy_r.at[d - 1, c], at_y(d),
            )

    def u_own(c):
        for d in (1, 3, 2):
            u_x[d, 0, c] = send(
                u_in.at[0, 2 * y + c, 0], ubuf.at[c, x, y],
                ux_s.at[d - 1, 0, c], ux_r.at[d - 1, 0, c], at_x(d),
            )

    def u_pass(c):
        for k in (1, 3, 2):
            u_y[k, c].wait_recv()
            piece = ubuf.at[c, x, from_y[k]]
            for d in (1, 3, 2):
                u_x[d, k, c] = send(
                    piece, piece, ux_s.at[d - 1, k, c], ux_r.at[d - 1, k, c], at_x(d)
                )

    zc = {}

    def z_send(rel, k, down, src=None):
        piece = from_y[k]
        src = lbuf.at[rel, piece] if src is None else src
        if down:
            to = rel + 1
            zc[to, k] = send(src, lbuf.at[to, piece], zm_s.at[rel, k], z_r.at[to, k], at_z(-1))
        else:
            to = (rel + NZ - 1) % NZ
            zc[to, k] = send(src, lbuf.at[to, piece], zp_s.at[rel, k], z_r.at[to, k], at_z(1))

    def z_pass(step, pieces=(1, 3, 2)):
        for k in pieces:
            for rel, down in ((step, True), (NZ - step, False)):
                zc[rel, k].wait_recv()
                if step < 3 or down == (k in (0, 2)):
                    z_send(rel, k, down)

    lane = lax.broadcasted_iota(jnp.int32, (1, 128), 1)

    def column_hots():
        col_ids = lax.broadcasted_iota(jnp.int32, (256, 128), 0)
        for h in range(8):
            single = umap[h]
            both = jnp.concatenate([single, single], axis=1)
            target = jnp.where(lane < 64, jnp.where(both < 128, both, -1), both + 128)
            col_hot[h] = (col_ids == target).astype(F32).astype(BF16)

    shift = lax.rem(NZ - z, NZ) * 64

    def row_hots(tiles):
        for tile in tiles:
            d, c = divmod(tile, 2)
            turned = pltpu.roll(lmap[2 * from_y[d] + c], shift, 1)
            t = [turned[:, 128 * i : 128 * i + 128] for i in range(4)]
            rows = (t[0], jnp.where(lane < 64, t[1], t[3]), jnp.where(lane < 64, t[3], t[1]), t[2])

            def fill(step, carry):
                base = pl.multiple_of(step * 64, 64)
                ids = lax.broadcasted_iota(jnp.int32, (64, 128), 0) + base
                for g in range(4):
                    hot[g, pl.ds(base, 64), tile * 128 : tile * 128 + 128] = (
                        (ids == rows[g]).astype(F32).astype(BF16)
                    )
                return carry

            lax.fori_loop(0, 16, fill, 0)

    def u_join(c):
        for k in (0, 1, 3, 2):
            for d in (1, 3, 2):
                u_x[d, k, c].wait_recv()
        for q in range(NY):
            high, low = split(ubuf[c, :, q].reshape(64, 256))
            whi[c, 64 * q : 64 * q + 64] = high
            wlo[c, 64 * q : 64 * q + 64] = low

    rc = {}

    def multiply(g, children=(0, 1)):
        first, second = GROUPS[g]
        for c in children:
            left = jnp.concatenate(
                [lbuf[first, :, c].reshape(64, 256), lbuf[second, :, c].reshape(64, 256)], axis=0
            )
            high, low = split(left)
            prod = dot_nt(high, wlo[c]) + dot_nt(low, whi[c]) + dot_nt(high, whi[c])
            for j in range(2):
                top = prod[:64, 128 * j : 128 * j + 128]
                bottom = prod[64:, 128 * j : 128 * j + 128]
                packed[g, c, 2 * j] = jnp.where(lane < 64, top, pltpu.roll(bottom, 64, 1))
                packed[g, c, 2 * j + 1] = jnp.where(lane < 64, pltpu.roll(top, 64, 1), bottom)
            for d in (2, 1, 3):
                rc[g, c, d] = send(
                    packed.at[g, c, peer_y[d]], recv.at[g, c, d - 1],
                    res_s.at[g, c, d - 1], res_r.at[g, c, d - 1], at_y(d),
                )

    def expand(g):
        for d in (0, 1, 3, 2):
            for c in range(2):
                if d == 0:
                    value = packed[g, c, y]
                else:
                    rc[g, c, d].wait_recv()
                    value = recv[g, c, d - 1]
                high, low = split(value)
                wide = dot_nt(jnp.concatenate([high, low], axis=0), col_hot[2 * from_y[d] + c]).astype(BF16)
                at = (2 * d + c) * 128
                dense[at : at + 64, :128] = wide[:64, :128]
                dense[at + 64 : at + 128, :128] = wide[:64, 128:]
                dense[at : at + 64, 128:] = wide[64:, :128]
                dense[at + 64 : at + 128, 128:] = wide[64:, 128:]

    size = 1024 // CHUNKS

    def scatter(g, chunk):
        rows = slice(chunk * size, chunk * size + size)
        both = jnp.dot(hot[g, rows], dense[...], preferred_element_type=F32)
        return both[:, :128] + both[:, 128:]

    def update(g):
        expand(g)
        for chunk in range(CHUNKS):
            rows = slice(chunk * size, chunk * size + size)
            part = scatter(g, chunk)
            acc[rows] = part if g == 0 else acc[rows] + part

    for down in (True, False):
        z_send(0, 0, down, l_in.at[0, pl.ds(2 * y, 2), 0])
    u_spread(0)
    u_own(0)
    for d in (1, 3, 2):
        src = l_in.at[0, pl.ds(2 * peer_y[d], 2), 0]
        zc[1, d] = send(src, lbuf.at[1, y], ly_s.at[d - 1, 1], z_r.at[1, d], at_z(-1, d))
        zc[7, d] = send(src, lbuf.at[7, y], ly_s.at[d - 1, 2], z_r.at[7, d], at_z(1, d))
    u_spread(1)
    u_own(1)
    for d in (1, 3, 2):
        src = l_in.at[0, pl.ds(2 * peer_y[d], 2), 0]
        zc[0, d] = send(src, lbuf.at[0, y], ly_s.at[d - 1, 0], z_r.at[0, d], at_y(d))
    for copy in maps:
        copy.wait()
    row_hots((0,))
    z_pass(1, (0,))
    u_pass(0)
    z_pass(1)
    u_pass(1)
    z_pass(2, (0,))
    row_hots((1, 2))
    z_pass(2, (1,))
    z_pass(3, (0,))
    own_u.wait()
    own_l.wait()
    for d in (1, 3, 2):
        zc[0, d].wait_recv()
    u_join(0)
    multiply(0, (0,))
    z_pass(2, (3, 2))
    u_join(1)
    multiply(0, (1,))
    z_pass(3, (1,))
    multiply(1)
    z_pass(3, (3, 2))
    multiply(2)
    row_hots((3, 4, 5, 6, 7))
    column_hots()
    update(0)
    for k in (0, 1, 3, 2):
        zc[4, k].wait_recv()
    multiply(3)
    update(1)
    update(2)
    expand(3)
    ex = []
    for chunk in range(CHUNKS):
        rows = slice(chunk * size, chunk * size + size)
        mine[rows] = acc[rows] + scatter(3, chunk)
        ex.append(send(mine.at[rows], other.at[rows], ex_s.at[chunk], ex_r.at[chunk], twin))
    fetch.wait()
    for chunk in range(CHUNKS):
        rows = slice(chunk * size, chunk * size + size)
        ex[chunk].wait_recv()
        out[rows] = front_v[rows] - (mine[rows] + other[rows])
    for copy in sent:
        copy.wait_send()


def shards(front_matrix, l_panels, l_map, u_panels, u_map):
    hbm = pl.BlockSpec(memory_space=pltpu.HBM)
    operands = [
        pltpu.with_memory_space_constraint(operand, pltpu.HBM)
        for operand in (front_matrix, l_panels, l_map, u_panels, u_map)
    ]
    vmem = pl.BlockSpec(memory_space=pltpu.VMEM)
    dma = pltpu.SemaphoreType.DMA
    return pl.pallas_call(
        kernel,
        out_shape=jax.ShapeDtypeStruct((1024, 128), F32),
        in_specs=[hbm] * 5,
        out_specs=vmem,
        scratch_shapes=[
            pltpu.VMEM((NZ, NY, 2, 16, 256), F32),
            pltpu.VMEM((2, NX, NY, 16, 256), F32),
            pltpu.VMEM((2, 256, 256), BF16),
            pltpu.VMEM((2, 256, 256), BF16),
            pltpu.VMEM((4, 1024, 1024), BF16),
            pltpu.VMEM((8, 256, 128), BF16),
            pltpu.VMEM((4, 2, NY, 64, 128), F32),
            pltpu.VMEM((4, 2, 3, 64, 128), F32),
            pltpu.VMEM((1024, 256), BF16),
            pltpu.VMEM((1024, 128), F32),
            pltpu.VMEM((1024, 128), F32),
            pltpu.VMEM((1024, 128), F32),
            pltpu.VMEM((1024, 128), F32),
            pltpu.VMEM((8, 1, 512), jnp.int32),
            pltpu.VMEM((8, 1, 64), jnp.int32),
            dma((3, 2)), dma((3, 2)), dma((3, 4, 2)), dma((3, 4, 2)), dma((3, 3)),
            dma((NZ, 4)), dma((NZ, 4)), dma((NZ, 4)),
            dma((4, 2, 3)), dma((4, 2, 3)), dma((CHUNKS,)), dma((CHUNKS,)), dma((5,)),
        ],
        compiler_params=pltpu.CompilerParams(
            collective_id=0, has_side_effects=True, vmem_limit_bytes=48 << 20
        ),
        name="extend_add",
    )(*operands)


def solution(mesh):
    placed = (
        P("row", "col"),
        P("gz", None, "row", "col", None),
        P("gz", None, "row", None),
        P("gz", None, "col", "row", None),
        P("gz", None, "col", None),
    )
    return jax.shard_map(
        shards, mesh=mesh, in_specs=placed, out_specs=P("row", "col"), check_vma=False
    )
```

```python
import functools

import jax
import jax.numpy as jnp
from jax import lax
from jax.experimental import pallas as pl
from jax.experimental.pallas import tpu as pltpu
from jax.sharding import PartitionSpec as P

MESH = pl.DeviceIdType.MESH
F32 = jnp.float32
BF16 = jnp.bfloat16
NX, NY, NZ = 4, 4, 8
GROUPS = ((0, 1), (2, 7), (6, 3), (4, 5))
CHUNKS = 4


def split(value):
    high = value.astype(BF16)
    return high, (value - high.astype(F32)).astype(BF16)


def dot_nt(left, right):
    return lax.dot_general(left, right, (((1,), (1,)), ((), ())), preferred_element_type=F32)


def kernel(
    front, l_in, lmap_in, u_in, umap_in, out,
    lbuf, ubuf, whi, wlo, hot, col_hot, packed, recv, dense, acc, mine, other, front_v, lmap, umap,
    uy_s, uy_r, ux_s, ux_r, ly_s, z_s, z_r, res_s, res_r, ex_s, ex_r, loc,
):
    core, x, col = lax.axis_index("gz"), lax.axis_index("row"), lax.axis_index("col")
    y, z = lax.rem(col, NY), lax.div(col, NY)
    peer_y = [lax.rem(y + d, NY) for d in range(NY)]
    from_y = [lax.rem(y + NY - d, NY) for d in range(NY)]

    def at_y(d):
        return (core, x, z * NY + peer_y[d])

    def at_x(d):
        return (core, lax.rem(x + d, NX), col)

    def at_z(d, dy=0):
        return (core, x, lax.rem(z + NZ + d, NZ) * NY + peer_y[dy])

    twin = (1 - core, x, col)
    peers = [at_y(d) for d in (1, 2, 3)] + [at_x(d) for d in (1, 2, 3)] + [twin]
    peers += [at_z(d, dy) for d in (1, -1, 2, -2) for dy in range(NY)]
    barrier = pltpu.get_barrier_semaphore()
    for peer in peers:
        pl.semaphore_signal(barrier, inc=1, device_id=peer, device_id_type=MESH)
    fetch = pltpu.make_async_copy(front, front_v, loc.at[0])
    own_l = pltpu.make_async_copy(l_in.at[0, pl.ds(2 * y, 2), 0], lbuf.at[0, y], loc.at[1])
    maps = (
        pltpu.make_async_copy(lmap_in.at[0], lmap, loc.at[3]),
        pltpu.make_async_copy(umap_in.at[0], umap, loc.at[4]),
    )
    own_u = pltpu.make_async_copy(u_in.at[0, pl.ds(2 * y, 2), 0], ubuf.at[:, x, y], loc.at[2])
    for copy in maps:
        copy.start()
    fetch.start()
    own_l.start()
    own_u.start()
    pl.semaphore_wait(barrier, len(peers))

    sent = []

    def send(src, dst, send_sem, recv_sem, device):
        copy = pltpu.make_async_remote_copy(
            src_ref=src, dst_ref=dst, send_sem=send_sem, recv_sem=recv_sem,
            device_id=device, device_id_type=MESH,
        )
        copy.start()
        sent.append(copy)
        return copy

    u_y, u_x = {}, {}

    def u_spread(c):
        for d in (1, 3, 2):
            u_y[d, c] = send(
                u_in.at[0, 2 * peer_y[d] + c, 0], ubuf.at[c, x, y],
                uy_s.at[d - 1, c], uy_r.at[d - 1, c], at_y(d),
            )

    def u_own(c):
        for d in (1, 3, 2):
            u_x[d, 0, c] = send(
                u_in.at[0, 2 * y + c, 0], ubuf.at[c, x, y],
                ux_s.at[d - 1, 0, c], ux_r.at[d - 1, 0, c], at_x(d),
            )

    def u_pass(c):
        for k in (1, 3, 2):
            u_y[k, c].wait_recv()
            piece = ubuf.at[c, x, from_y[k]]
            for d in (1, 3, 2):
                u_x[d, k, c] = send(
                    piece, piece, ux_s.at[d - 1, k, c], ux_r.at[d - 1, k, c], at_x(d)
                )

    zc = {}

    def z_start(reach, distances):
        for d in distances:
            src = l_in.at[0, pl.ds(2 * peer_y[d], 2), 0]
            for dz in (-reach, reach):
                rel = (-dz) % NZ
                zc[rel, d] = send(src, lbuf.at[rel, y], z_s.at[rel, d], z_r.at[rel, d], at_z(dz, d))

    def z_pass(step, pieces=(1, 3, 2)):
        for k in pieces:
            for rel, dz in ((step, -1), (NZ - step, 1)):
                zc[rel, k].wait_recv()
                if step == 2 or (step == 3 and (dz < 0) == (k in (0, 2))):
                    to = rel - dz
                    slot = to if to != 4 else (4 if dz < 0 else 0)
                    zc[to, k] = send(
                        lbuf.at[rel, from_y[k]], lbuf.at[to, from_y[k]],
                        z_s.at[slot, k], z_r.at[to, k], at_z(dz),
                    )

    lane = lax.broadcasted_iota(jnp.int32, (1, 128), 1)

    def column_hots():
        col_ids = lax.broadcasted_iota(jnp.int32, (256, 128), 0)
        for h in range(8):
            single = umap[h]
            both = jnp.concatenate([single, single], axis=1)
            target = jnp.where(lane < 64, jnp.where(both < 128, both, -1), both + 128)
            col_hot[h] = (col_ids == target).astype(F32).astype(BF16)

    shift = lax.rem(NZ - z, NZ) * 64

    def row_hots(tiles):
        for tile in tiles:
            d, c = divmod(tile, 2)
            turned = pltpu.roll(lmap[2 * from_y[d] + c], shift, 1)
            t = [turned[:, 128 * i : 128 * i + 128] for i in range(4)]
            rows = (t[0], jnp.where(lane < 64, t[1], t[3]), jnp.where(lane < 64, t[3], t[1]), t[2])

            def fill(step, carry):
                base = pl.multiple_of(step * 64, 64)
                ids = lax.broadcasted_iota(jnp.int32, (64, 128), 0) + base
                for g in range(4):
                    hot[g, pl.ds(base, 64), tile * 128 : tile * 128 + 128] = (
                        (ids == rows[g]).astype(F32).astype(BF16)
                    )
                return carry

            lax.fori_loop(0, 16, fill, 0)

    def u_join(c):
        for k in (0, 1, 3, 2):
            for d in (1, 3, 2):
                u_x[d, k, c].wait_recv()
        for q in range(NY):
            high, low = split(ubuf[c, :, q].reshape(64, 256))
            whi[c, 64 * q : 64 * q + 64] = high
            wlo[c, 64 * q : 64 * q + 64] = low

    rc = {}

    def multiply(g, children=(0, 1)):
        first, second = GROUPS[g]
        for c in children:
            left = jnp.concatenate(
                [lbuf[first, :, c].reshape(64, 256), lbuf[second, :, c].reshape(64, 256)], axis=0
            )
            high, low = split(left)
            prod = dot_nt(high, wlo[c]) + dot_nt(low, whi[c]) + dot_nt(high, whi[c])
            for j in range(2):
                top = prod[:64, 128 * j : 128 * j + 128]
                bottom = prod[64:, 128 * j : 128 * j + 128]
                packed[g, c, 2 * j] = jnp.where(lane < 64, top, pltpu.roll(bottom, 64, 1))
                packed[g, c, 2 * j + 1] = jnp.where(lane < 64, pltpu.roll(top, 64, 1), bottom)
            for d in (1, 3, 2):
                rc[g, c, d] = send(
                    packed.at[g, c, peer_y[d]], recv.at[g, c, d - 1],
                    res_s.at[g, c, d - 1], res_r.at[g, c, d - 1], at_y(d),
                )

    def expand(g):
        for d in (0, 1, 3, 2):
            for c in range(2):
                if d == 0:
                    value = packed[g, c, y]
                else:
                    rc[g, c, d].wait_recv()
                    value = recv[g, c, d - 1]
                high, low = split(value)
                wide = dot_nt(jnp.concatenate([high, low], axis=0), col_hot[2 * from_y[d] + c]).astype(BF16)
                at = (2 * d + c) * 128
                dense[at : at + 64, :128] = wide[:64, :128]
                dense[at + 64 : at + 128, :128] = wide[:64, 128:]
                dense[at : at + 64, 128:] = wide[64:, :128]
                dense[at + 64 : at + 128, 128:] = wide[64:, 128:]

    size = 1024 // CHUNKS

    def scatter(g, chunk):
        rows = slice(chunk * size, chunk * size + size)
        both = jnp.dot(hot[g, rows], dense[...], preferred_element_type=F32)
        return both[:, :128] + both[:, 128:]

    def update(g):
        expand(g)
        for chunk in range(CHUNKS):
            rows = slice(chunk * size, chunk * size + size)
            part = scatter(g, chunk)
            acc[rows] = part if g == 0 else acc[rows] + part

    z_start(1, (0,))
    z_start(2, (0,))
    u_spread(0)
    u_own(0)
    z_start(2, (1, 3, 2))
    u_spread(1)
    u_own(1)
    z_start(1, (1, 3, 2))
    for d in (1, 3, 2):
        src = l_in.at[0, pl.ds(2 * peer_y[d], 2), 0]
        zc[0, d] = send(src, lbuf.at[0, y], ly_s.at[d - 1], z_r.at[0, d], at_y(d))
    for copy in maps:
        copy.wait()
    row_hots((0, 1, 2))
    z_pass(2, (0,))
    u_pass(0)
    u_pass(1)
    z_pass(2)
    z_pass(3, (0,))
    own_u.wait()
    own_l.wait()
    for d in (1, 3, 2):
        zc[0, d].wait_recv()
    z_pass(1, (0, 1, 3, 2))
    u_join(0)
    multiply(0, (0,))
    z_pass(3, (1,))
    u_join(1)
    multiply(0, (1,))
    multiply(1)
    z_pass(3, (3, 2))
    multiply(2)
    row_hots((3, 4, 5, 6, 7))
    column_hots()
    update(0)
    for k in (0, 1, 3, 2):
        zc[4, k].wait_recv()
    multiply(3)
    update(1)
    update(2)
    expand(3)
    ex = []
    for chunk in range(CHUNKS):
        rows = slice(chunk * size, chunk * size + size)
        mine[rows] = acc[rows] + scatter(3, chunk)
        ex.append(send(mine.at[rows], other.at[rows], ex_s.at[chunk], ex_r.at[chunk], twin))
    fetch.wait()
    for chunk in range(CHUNKS):
        rows = slice(chunk * size, chunk * size + size)
        ex[chunk].wait_recv()
        out[rows] = front_v[rows] - (mine[rows] + other[rows])
    for copy in sent:
        copy.wait_send()


def shards(front_matrix, l_panels, l_map, u_panels, u_map):
    hbm = pl.BlockSpec(memory_space=pltpu.HBM)
    operands = [
        pltpu.with_memory_space_constraint(operand, pltpu.HBM)
        for operand in (front_matrix, l_panels, l_map, u_panels, u_map)
    ]
    vmem = pl.BlockSpec(memory_space=pltpu.VMEM)
    dma = pltpu.SemaphoreType.DMA
    return pl.pallas_call(
        kernel,
        out_shape=jax.ShapeDtypeStruct((1024, 128), F32),
        in_specs=[hbm] * 5,
        out_specs=vmem,
        scratch_shapes=[
            pltpu.VMEM((NZ, NY, 2, 16, 256), F32),
            pltpu.VMEM((2, NX, NY, 16, 256), F32),
            pltpu.VMEM((2, 256, 256), BF16),
            pltpu.VMEM((2, 256, 256), BF16),
            pltpu.VMEM((4, 1024, 1024), BF16),
            pltpu.VMEM((8, 256, 128), BF16),
            pltpu.VMEM((4, 2, NY, 64, 128), F32),
            pltpu.VMEM((4, 2, 3, 64, 128), F32),
            pltpu.VMEM((1024, 256), BF16),
            pltpu.VMEM((1024, 128), F32),
            pltpu.VMEM((1024, 128), F32),
            pltpu.VMEM((1024, 128), F32),
            pltpu.VMEM((1024, 128), F32),
            pltpu.VMEM((8, 1, 512), jnp.int32),
            pltpu.VMEM((8, 1, 64), jnp.int32),
            dma((3, 2)), dma((3, 2)), dma((3, 4, 2)), dma((3, 4, 2)), dma((3,)),
            dma((NZ, 4)), dma((NZ, 4)),
            dma((4, 2, 3)), dma((4, 2, 3)), dma((CHUNKS,)), dma((CHUNKS,)), dma((5,)),
        ],
        compiler_params=pltpu.CompilerParams(
            collective_id=0, has_side_effects=True, vmem_limit_bytes=48 << 20
        ),
        name="extend_add",
    )(*operands)


def solution(mesh):
    placed = (
        P("row", "col"),
        P("gz", None, "row", "col", None),
        P("gz", None, "row", None),
        P("gz", None, "col", "row", None),
        P("gz", None, "col", None),
    )
    return jax.shard_map(
        shards, mesh=mesh, in_specs=placed, out_specs=P("row", "col"), check_vma=False
    )
```

```python
import functools

import jax
import jax.numpy as jnp
from jax import lax
from jax.experimental import pallas as pl
from jax.experimental.pallas import tpu as pltpu
from jax.sharding import PartitionSpec as P

MESH = pl.DeviceIdType.MESH
F32 = jnp.float32
BF16 = jnp.bfloat16
NX, NY, NZ = 4, 4, 8
GROUPS = ((0, 1), (2, 7), (6, 3), (4, 5))
CHUNKS = 2


def split(value):
    high = value.astype(BF16)
    return high, (value - high.astype(F32)).astype(BF16)


def dot_nt(left, right):
    return lax.dot_general(left, right, (((1,), (1,)), ((), ())), preferred_element_type=F32)


def kernel(
    front, l_in, lmap_in, u_in, umap_in, out,
    lbuf, ubuf, whi, wlo, hot, col_hot, packed, recv, dense, acc, other, front_v, lmap, umap,
    uy_s, uy_r, ux_s, ux_r, ly_s, z_s, z_r, res_s, res_r, ex_s, ex_r, loc,
):
    core, x, col = lax.axis_index("gz"), lax.axis_index("row"), lax.axis_index("col")
    y, z = lax.rem(col, NY), lax.div(col, NY)
    turn = 1 - 2 * core
    peer_y = [lax.rem(y + NY + turn * d, NY) for d in range(NY)]
    from_y = [lax.rem(y + NY - turn * d, NY) for d in range(NY)]

    def at_y(d):
        return (core, x, z * NY + peer_y[d])

    def at_x(d):
        return (core, lax.rem(x + NX + turn * d, NX), col)

    def at_z(d, dy=0):
        return (core, x, lax.rem(z + NZ + d, NZ) * NY + peer_y[dy])

    twin = (1 - core, x, col)
    peers = [at_y(d) for d in (1, 2, 3)] + [at_x(d) for d in (1, 2, 3)] + [twin]
    peers += [at_z(d, dy) for d in (1, -1, 2, -2) for dy in range(NY)]
    barrier = pltpu.get_barrier_semaphore()
    for peer in peers:
        pl.semaphore_signal(barrier, inc=1, device_id=peer, device_id_type=MESH)
    fetch = pltpu.make_async_copy(front, front_v, loc.at[0])
    own_l = pltpu.make_async_copy(l_in.at[0, pl.ds(2 * y, 2), 0], lbuf.at[0, y], loc.at[1])
    maps = (
        pltpu.make_async_copy(lmap_in.at[0], lmap, loc.at[3]),
        pltpu.make_async_copy(umap_in.at[0], umap, loc.at[4]),
    )
    own_u = pltpu.make_async_copy(u_in.at[0, pl.ds(2 * y, 2), 0], ubuf.at[:, x, y], loc.at[2])
    for copy in maps:
        copy.start()
    fetch.start()
    own_l.start()
    own_u.start()
    pl.semaphore_wait(barrier, len(peers))

    sent = []

    def send(src, dst, send_sem, recv_sem, device):
        copy = pltpu.make_async_remote_copy(
            src_ref=src, dst_ref=dst, send_sem=send_sem, recv_sem=recv_sem,
            device_id=device, device_id_type=MESH,
        )
        copy.start()
        sent.append(copy)
        return copy

    u_y, u_x = {}, {}

    def u_spread(c):
        for d in (1, 3, 2):
            u_y[d, c] = send(
                u_in.at[0, 2 * peer_y[d] + c, 0], ubuf.at[c, x, y],
                uy_s.at[d - 1, c], uy_r.at[d - 1, c], at_y(d),
            )

    def u_own(c):
        for d in (1, 3, 2):
            u_x[d, 0, c] = send(
                u_in.at[0, 2 * y + c, 0], ubuf.at[c, x, y],
                ux_s.at[d - 1, 0, c], ux_r.at[d - 1, 0, c], at_x(d),
            )

    def u_pass(c):
        for k in (1, 3, 2):
            u_y[k, c].wait_recv()
            piece = ubuf.at[c, x, from_y[k]]
            for d in (1, 3, 2):
                u_x[d, k, c] = send(
                    piece, piece, ux_s.at[d - 1, k, c], ux_r.at[d - 1, k, c], at_x(d)
                )

    zc = {}

    def z_start(reach, distances):
        for d in distances:
            src = l_in.at[0, pl.ds(2 * peer_y[d], 2), 0]
            for dz in (-reach, reach):
                rel = (-dz) % NZ
                zc[rel, d] = send(src, lbuf.at[rel, y], z_s.at[rel, d], z_r.at[rel, d], at_z(dz, d))

    def z_pass(step, pieces=(1, 3, 2)):
        for k in pieces:
            for rel, dz in ((step, -1), (NZ - step, 1)):
                zc[rel, k].wait_recv()
                if step == 2 or (step == 3 and (dz < 0) == (k in (0, 2))):
                    to = rel - dz
                    slot = to if to != 4 else (4 if dz < 0 else 0)
                    zc[to, k] = send(
                        lbuf.at[rel, from_y[k]], lbuf.at[to, from_y[k]],
                        z_s.at[slot, k], z_r.at[to, k], at_z(dz),
                    )

    lane = lax.broadcasted_iota(jnp.int32, (1, 128), 1)

    def column_hots():
        col_ids = lax.broadcasted_iota(jnp.int32, (256, 128), 0)
        for h in range(8):
            single = umap[h]
            both = jnp.concatenate([single, single], axis=1)
            target = jnp.where(lane < 64, jnp.where(both < 128, both, -1), both + 128)
            col_hot[h] = (col_ids == target).astype(F32).astype(BF16)

    shift = lax.rem(NZ - z, NZ) * 64

    def row_hots(tiles):
        for tile in tiles:
            d, c = divmod(tile, 2)
            turned = pltpu.roll(lmap[2 * from_y[d] + c], shift, 1)
            t = [turned[:, 128 * i : 128 * i + 128] for i in range(4)]
            rows = (t[0], jnp.where(lane < 64, t[1], t[3]), jnp.where(lane < 64, t[3], t[1]), t[2])

            def fill(step, carry):
                base = pl.multiple_of(step * 64, 64)
                ids = lax.broadcasted_iota(jnp.int32, (64, 128), 0) + base
                for g in range(4):
                    hot[g, pl.ds(base, 64), tile * 128 : tile * 128 + 128] = (
                        (ids == rows[g]).astype(F32).astype(BF16)
                    )
                return carry

            lax.fori_loop(0, 16, fill, 0)

    def u_join(c):
        for k in (0, 1, 3, 2):
            for d in (1, 3, 2):
                u_x[d, k, c].wait_recv()
        for q in range(NY):
            high, low = split(ubuf[c, :, q].reshape(64, 256))
            whi[c, 64 * q : 64 * q + 64] = high
            wlo[c, 64 * q : 64 * q + 64] = low

    rc = {}

    def multiply(g, children=(0, 1)):
        first, second = GROUPS[g]
        for c in children:
            left = jnp.concatenate(
                [lbuf[first, :, c].reshape(64, 256), lbuf[second, :, c].reshape(64, 256)], axis=0
            )
            high, low = split(left)
            prod = dot_nt(high, wlo[c]) + dot_nt(low, whi[c]) + dot_nt(high, whi[c])
            for j in range(2):
                top = prod[:64, 128 * j : 128 * j + 128]
                bottom = prod[64:, 128 * j : 128 * j + 128]
                packed[g, c, 2 * j] = jnp.where(lane < 64, top, pltpu.roll(bottom, 64, 1))
                packed[g, c, 2 * j + 1] = jnp.where(lane < 64, pltpu.roll(top, 64, 1), bottom)
            for d in (1, 3, 2):
                rc[g, c, d] = send(
                    packed.at[g, c, peer_y[d]], recv.at[g, c, d - 1],
                    res_s.at[g, c, d - 1], res_r.at[g, c, d - 1], at_y(d),
                )

    def expand(g):
        for d in (0, 1, 3, 2):
            for c in range(2):
                if d == 0:
                    value = packed[g, c, y]
                else:
                    rc[g, c, d].wait_recv()
                    value = recv[g, c, d - 1]
                high, low = split(value)
                wide = dot_nt(jnp.concatenate([high, low], axis=0), col_hot[2 * from_y[d] + c]).astype(BF16)
                at = (2 * d + c) * 128
                dense[at : at + 64, :128] = wide[:64, :128]
                dense[at + 64 : at + 128, :128] = wide[:64, 128:]
                dense[at : at + 64, 128:] = wide[64:, :128]
                dense[at + 64 : at + 128, 128:] = wide[64:, 128:]

    size = 1024 // CHUNKS

    def scatter(g, chunk):
        rows = slice(chunk * size, chunk * size + size)
        both = jnp.dot(hot[g, rows], dense[...], preferred_element_type=F32)
        return both[:, :128] + both[:, 128:]

    lowest = [jnp.minimum(lax.rem(z + i, NZ), lax.rem(z + j, NZ)) * 128 for i, j in GROUPS]

    def add_rows(g, chunk):
        rows = slice(chunk * size, chunk * size + size)
        if g == 0:
            acc[rows] = scatter(g, chunk)
            return

        @pl.when(lowest[g] < chunk * size + size)
        def _():
            acc[rows] += scatter(g, chunk)

    def update(g):
        expand(g)
        for chunk in range(CHUNKS):
            add_rows(g, chunk)

    z_start(1, (0,))
    z_start(2, (0,))
    u_spread(0)
    u_own(0)
    z_start(2, (1, 3, 2))
    u_spread(1)
    u_own(1)
    z_start(1, (1, 3, 2))
    for d in (1, 3, 2):
        src = l_in.at[0, pl.ds(2 * peer_y[d], 2), 0]
        zc[0, d] = send(src, lbuf.at[0, y], ly_s.at[d - 1], z_r.at[0, d], at_y(d))
    for copy in maps:
        copy.wait()
    row_hots((0, 1, 2))
    z_pass(2, (0,))
    u_pass(0)
    u_pass(1)
    z_pass(2)
    z_pass(3, (0,))
    own_u.wait()
    own_l.wait()
    for d in (1, 3, 2):
        zc[0, d].wait_recv()
    z_pass(1, (0, 1, 3, 2))
    u_join(0)
    multiply(0, (0,))
    z_pass(3, (1,))
    u_join(1)
    multiply(0, (1,))
    multiply(1)
    z_pass(3, (3, 2))
    multiply(2)
    row_hots((3, 4, 5, 6, 7))
    column_hots()
    update(0)
    for k in (0, 1, 3, 2):
        zc[4, k].wait_recv()
    multiply(3)
    update(1)
    update(2)
    expand(3)
    ex = []
    for chunk in range(CHUNKS):
        rows = slice(chunk * size, chunk * size + size)
        add_rows(3, chunk)
        ex.append(send(acc.at[rows], other.at[rows], ex_s.at[chunk], ex_r.at[chunk], twin))
    fetch.wait()
    for chunk in range(CHUNKS):
        rows = slice(chunk * size, chunk * size + size)
        ex[chunk].wait_recv()
        out[rows] = front_v[rows] - (acc[rows] + other[rows])
    for copy in sent:
        copy.wait_send()


def shards(front_matrix, l_panels, l_map, u_panels, u_map):
    hbm = pl.BlockSpec(memory_space=pltpu.HBM)
    operands = [
        pltpu.with_memory_space_constraint(operand, pltpu.HBM)
        for operand in (front_matrix, l_panels, l_map, u_panels, u_map)
    ]
    vmem = pl.BlockSpec(memory_space=pltpu.VMEM)
    dma = pltpu.SemaphoreType.DMA
    return pl.pallas_call(
        kernel,
        out_shape=jax.ShapeDtypeStruct((1024, 128), F32),
        in_specs=[hbm] * 5,
        out_specs=vmem,
        scratch_shapes=[
            pltpu.VMEM((NZ, NY, 2, 16, 256), F32),
            pltpu.VMEM((2, NX, NY, 16, 256), F32),
            pltpu.VMEM((2, 256, 256), BF16),
            pltpu.VMEM((2, 256, 256), BF16),
            pltpu.VMEM((4, 1024, 1024), BF16),
            pltpu.VMEM((8, 256, 128), BF16),
            pltpu.VMEM((4, 2, NY, 64, 128), F32),
            pltpu.VMEM((4, 2, 3, 64, 128), F32),
            pltpu.VMEM((1024, 256), BF16),
            pltpu.VMEM((1024, 128), F32),
            pltpu.VMEM((1024, 128), F32),
            pltpu.VMEM((1024, 128), F32),
            pltpu.VMEM((8, 1, 512), jnp.int32),
            pltpu.VMEM((8, 1, 64), jnp.int32),
            dma((3, 2)), dma((3, 2)), dma((3, 4, 2)), dma((3, 4, 2)), dma((3,)),
            dma((NZ, 4)), dma((NZ, 4)),
            dma((4, 2, 3)), dma((4, 2, 3)), dma((CHUNKS,)), dma((CHUNKS,)), dma((5,)),
        ],
        compiler_params=pltpu.CompilerParams(
            collective_id=0, has_side_effects=True, vmem_limit_bytes=48 << 20
        ),
        name="extend_add",
    )(*operands)


def solution(mesh):
    placed = (
        P("row", "col"),
        P("gz", None, "row", "col", None),
        P("gz", None, "row", None),
        P("gz", None, "col", "row", None),
        P("gz", None, "col", None),
    )
    return jax.shard_map(
        shards, mesh=mesh, in_specs=placed, out_specs=P("row", "col"), check_vma=False
    )
```

```python
import functools

import jax
import jax.numpy as jnp
from jax import lax
from jax.experimental import pallas as pl
from jax.experimental.pallas import tpu as pltpu
from jax.sharding import PartitionSpec as P

MESH = pl.DeviceIdType.MESH
F32 = jnp.float32
BF16 = jnp.bfloat16
NX, NY, NZ = 4, 4, 8
GROUPS = ((0, 1), (2, 7), (6, 3), (4, 5))
CHUNKS = 2


def split(value):
    high = value.astype(BF16)
    return high, (value - high.astype(F32)).astype(BF16)


def dot_nt(left, right):
    return lax.dot_general(left, right, (((1,), (1,)), ((), ())), preferred_element_type=F32)


def kernel(
    front, l_in, lmap_in, u_in, umap_in, out,
    lbuf, ubuf, whi, wlo, hot, col_hot, packed, recv, dense, acc, other, front_v, lmap, umap,
    uy_s, uy_r, ux_s, ux_r, ly_s, z_s, z_r, res_s, res_r, ex_s, ex_r, loc,
):
    core, x, col = lax.axis_index("gz"), lax.axis_index("row"), lax.axis_index("col")
    y, z = lax.rem(col, NY), lax.div(col, NY)
    turn = 1 - 2 * core
    peer_y = [lax.rem(y + NY + turn * d, NY) for d in range(NY)]
    from_y = [lax.rem(y + NY - turn * d, NY) for d in range(NY)]

    def at_y(d):
        return (core, x, z * NY + peer_y[d])

    def at_x(d):
        return (core, lax.rem(x + NX + turn * d, NX), col)

    def at_z(d, dy=0):
        return (core, x, lax.rem(z + NZ + d, NZ) * NY + peer_y[dy])

    twin = (1 - core, x, col)
    peers = [at_y(d) for d in (1, 2, 3)] + [at_x(d) for d in (1, 2, 3)] + [twin]
    peers += [at_z(d, dy) for d in (1, -1, 2, -2) for dy in range(NY)]
    barrier = pltpu.get_barrier_semaphore()
    for peer in peers:
        pl.semaphore_signal(barrier, inc=1, device_id=peer, device_id_type=MESH)
    fetch = pltpu.make_async_copy(front, front_v, loc.at[0])
    own_l = pltpu.make_async_copy(l_in.at[0, pl.ds(2 * y, 2), 0], lbuf.at[0, y], loc.at[1])
    maps = (
        pltpu.make_async_copy(lmap_in.at[0], lmap, loc.at[3]),
        pltpu.make_async_copy(umap_in.at[0], umap, loc.at[4]),
    )
    own_u = pltpu.make_async_copy(u_in.at[0, pl.ds(2 * y, 2), 0], ubuf.at[:, x, y], loc.at[2])
    for copy in maps:
        copy.start()
    fetch.start()
    own_l.start()
    own_u.start()
    pl.semaphore_wait(barrier, len(peers))

    sent = []

    def send(src, dst, send_sem, recv_sem, device):
        copy = pltpu.make_async_remote_copy(
            src_ref=src, dst_ref=dst, send_sem=send_sem, recv_sem=recv_sem,
            device_id=device, device_id_type=MESH,
        )
        copy.start()
        sent.append(copy)
        return copy

    u_y, u_x = {}, {}

    def u_spread(c):
        for d in (1, 3, 2):
            u_y[d, c] = send(
                u_in.at[0, 2 * peer_y[d] + c, 0], ubuf.at[c, x, y],
                uy_s.at[d - 1, c], uy_r.at[d - 1, c], at_y(d),
            )

    def u_own(c):
        for d in (1, 3, 2):
            u_x[d, 0, c] = send(
                u_in.at[0, 2 * y + c, 0], ubuf.at[c, x, y],
                ux_s.at[d - 1, 0, c], ux_r.at[d - 1, 0, c], at_x(d),
            )

    def u_pass(c):
        for k in (1, 3, 2):
            u_y[k, c].wait_recv()
            piece = ubuf.at[c, x, from_y[k]]
            for d in (1, 3, 2):
                u_x[d, k, c] = send(
                    piece, piece, ux_s.at[d - 1, k, c], ux_r.at[d - 1, k, c], at_x(d)
                )

    zc = {}

    def z_start(reach, distances):
        for d in distances:
            src = l_in.at[0, pl.ds(2 * peer_y[d], 2), 0]
            for dz in (-reach, reach):
                rel = (-dz) % NZ
                zc[rel, d] = send(src, lbuf.at[rel, y], z_s.at[rel, d], z_r.at[rel, d], at_z(dz, d))

    def z_pass(step, pieces=(1, 3, 2)):
        for k in pieces:
            for rel, dz in ((step, -1), (NZ - step, 1)):
                zc[rel, k].wait_recv()
                if step == 2 or (step == 3 and (dz < 0) == (k in (0, 2))):
                    to = rel - dz
                    slot = to if to != 4 else (4 if dz < 0 else 0)
                    zc[to, k] = send(
                        lbuf.at[rel, from_y[k]], lbuf.at[to, from_y[k]],
                        z_s.at[slot, k], z_r.at[to, k], at_z(dz),
                    )

    lane = lax.broadcasted_iota(jnp.int32, (1, 128), 1)

    def column_hots():
        col_ids = lax.broadcasted_iota(jnp.int32, (256, 128), 0)
        for h in range(8):
            single = umap[h]
            both = jnp.concatenate([single, single], axis=1)
            target = jnp.where(lane < 64, jnp.where(both < 128, both, -1), both + 128)
            col_hot[h] = (col_ids == target).astype(F32).astype(BF16)

    shift = lax.rem(NZ - z, NZ) * 64

    def row_hots(tiles):
        for tile in tiles:
            d, c = divmod(tile, 2)
            turned = pltpu.roll(lmap[2 * from_y[d] + c], shift, 1)
            t = [turned[:, 128 * i : 128 * i + 128] for i in range(4)]
            rows = (t[0], jnp.where(lane < 64, t[1], t[3]), jnp.where(lane < 64, t[3], t[1]), t[2])

            def fill(step, carry):
                base = pl.multiple_of(step * 64, 64)
                ids = lax.broadcasted_iota(jnp.int32, (64, 128), 0) + base
                for g in range(4):
                    hot[g, pl.ds(base, 64), tile * 128 : tile * 128 + 128] = (
                        (ids == rows[g]).astype(F32).astype(BF16)
                    )
                return carry

            lax.fori_loop(0, 16, fill, 0)

    def u_join(c):
        for k in (0, 1, 3, 2):
            for d in (1, 3, 2):
                u_x[d, k, c].wait_recv()
        for q in range(NY):
            high, low = split(ubuf[c, :, q].reshape(64, 256))
            whi[c, 64 * q : 64 * q + 64] = high
            wlo[c, 64 * q : 64 * q + 64] = low

    rc = {}

    def multiply(g, children=(0, 1)):
        first, second = GROUPS[g]
        for c in children:
            left = jnp.concatenate(
                [lbuf[first, :, c].reshape(64, 256), lbuf[second, :, c].reshape(64, 256)], axis=0
            )
            high, low = split(left)
            prod = dot_nt(high, wlo[c]) + dot_nt(low, whi[c]) + dot_nt(high, whi[c])
            for j in range(2):
                top = prod[:64, 128 * j : 128 * j + 128]
                bottom = prod[64:, 128 * j : 128 * j + 128]
                packed[g, c, 2 * j] = jnp.where(lane < 64, top, pltpu.roll(bottom, 64, 1))
                packed[g, c, 2 * j + 1] = jnp.where(lane < 64, pltpu.roll(top, 64, 1), bottom)
            for d in (2, 1, 3) if g == 3 else (1, 3, 2):
                rc[g, c, d] = send(
                    packed.at[g, c, peer_y[d]], recv.at[g, c, d - 1],
                    res_s.at[g, c, d - 1], res_r.at[g, c, d - 1], at_y(d),
                )

    def expand(g):
        for d in (0, 1, 3, 2):
            for c in range(2):
                if d == 0:
                    value = packed[g, c, y]
                else:
                    rc[g, c, d].wait_recv()
                    value = recv[g, c, d - 1]
                high, low = split(value)
                wide = dot_nt(jnp.concatenate([high, low], axis=0), col_hot[2 * from_y[d] + c]).astype(BF16)
                at = (2 * d + c) * 128
                dense[at : at + 64, :128] = wide[:64, :128]
                dense[at + 64 : at + 128, :128] = wide[:64, 128:]
                dense[at : at + 64, 128:] = wide[64:, :128]
                dense[at + 64 : at + 128, 128:] = wide[64:, 128:]

    size = 1024 // CHUNKS

    def scatter(g, chunk):
        rows = slice(chunk * size, chunk * size + size)
        both = jnp.dot(hot[g, rows], dense[...], preferred_element_type=F32)
        return both[:, :128] + both[:, 128:]

    lowest = [jnp.minimum(lax.rem(z + i, NZ), lax.rem(z + j, NZ)) * 128 for i, j in GROUPS]

    def add_rows(g, chunk):
        rows = slice(chunk * size, chunk * size + size)
        if g == 0:
            acc[rows] = scatter(g, chunk)
            return

        @pl.when(lowest[g] < chunk * size + size)
        def _():
            acc[rows] += scatter(g, chunk)

    def update(g):
        expand(g)
        for chunk in range(CHUNKS):
            add_rows(g, chunk)

    z_start(1, (0,))
    z_start(2, (0,))
    u_spread(0)
    u_own(0)
    z_start(2, (1, 3, 2))
    u_spread(1)
    u_own(1)
    z_start(1, (1, 3, 2))
    for d in (1, 3, 2):
        src = l_in.at[0, pl.ds(2 * peer_y[d], 2), 0]
        zc[0, d] = send(src, lbuf.at[0, y], ly_s.at[d - 1], z_r.at[0, d], at_y(d))
    for copy in maps:
        copy.wait()
    row_hots((0, 1, 2))
    z_pass(2, (0,))
    u_pass(0)
    u_pass(1)
    z_pass(2)
    z_pass(3, (0,))
    own_u.wait()
    own_l.wait()
    for d in (1, 3, 2):
        zc[0, d].wait_recv()
    z_pass(1, (0, 1, 3, 2))
    u_join(0)
    multiply(0, (0,))
    z_pass(3, (1,))
    u_join(1)
    multiply(0, (1,))
    multiply(1)
    z_pass(3, (3, 2))
    multiply(2)
    row_hots((3, 4, 5, 6, 7))
    column_hots()
    update(0)
    for k in (0, 1, 3, 2):
        zc[4, k].wait_recv()
    multiply(3)
    update(1)
    update(2)
    expand(3)
    ex = []
    for chunk in range(CHUNKS):
        rows = slice(chunk * size, chunk * size + size)
        add_rows(3, chunk)
        ex.append(send(acc.at[rows], other.at[rows], ex_s.at[chunk], ex_r.at[chunk], twin))
    fetch.wait()
    for chunk in range(CHUNKS):
        rows = slice(chunk * size, chunk * size + size)
        ex[chunk].wait_recv()
        out[rows] = front_v[rows] - (acc[rows] + other[rows])
    for copy in sent:
        copy.wait_send()


def shards(front_matrix, l_panels, l_map, u_panels, u_map):
    hbm = pl.BlockSpec(memory_space=pltpu.HBM)
    operands = [
        pltpu.with_memory_space_constraint(operand, pltpu.HBM)
        for operand in (front_matrix, l_panels, l_map, u_panels, u_map)
    ]
    vmem = pl.BlockSpec(memory_space=pltpu.VMEM)
    dma = pltpu.SemaphoreType.DMA
    return pl.pallas_call(
        kernel,
        out_shape=jax.ShapeDtypeStruct((1024, 128), F32),
        in_specs=[hbm] * 5,
        out_specs=vmem,
        scratch_shapes=[
            pltpu.VMEM((NZ, NY, 2, 16, 256), F32),
            pltpu.VMEM((2, NX, NY, 16, 256), F32),
            pltpu.VMEM((2, 256, 256), BF16),
            pltpu.VMEM((2, 256, 256), BF16),
            pltpu.VMEM((4, 1024, 1024), BF16),
            pltpu.VMEM((8, 256, 128), BF16),
            pltpu.VMEM((4, 2, NY, 64, 128), F32),
            pltpu.VMEM((4, 2, 3, 64, 128), F32),
            pltpu.VMEM((1024, 256), BF16),
            pltpu.VMEM((1024, 128), F32),
            pltpu.VMEM((1024, 128), F32),
            pltpu.VMEM((1024, 128), F32),
            pltpu.VMEM((8, 1, 512), jnp.int32),
            pltpu.VMEM((8, 1, 64), jnp.int32),
            dma((3, 2)), dma((3, 2)), dma((3, 4, 2)), dma((3, 4, 2)), dma((3,)),
            dma((NZ, 4)), dma((NZ, 4)),
            dma((4, 2, 3)), dma((4, 2, 3)), dma((CHUNKS,)), dma((CHUNKS,)), dma((5,)),
        ],
        compiler_params=pltpu.CompilerParams(
            collective_id=0, has_side_effects=True, vmem_limit_bytes=48 << 20
        ),
        name="extend_add",
    )(*operands)


def solution(mesh):
    placed = (
        P("row", "col"),
        P("gz", None, "row", "col", None),
        P("gz", None, "row", None),
        P("gz", None, "col", "row", None),
        P("gz", None, "col", None),
    )
    return jax.shard_map(
        shards, mesh=mesh, in_specs=placed, out_specs=P("row", "col"), check_vma=False
    )
```
